256 devices in a mesh: dp: 16 (over y_hi, x, core), expert: 16 (over y_lo, z).
Axes of the slice: x: 4, y: 4 (y_hi: 2, y_lo: 2; y = y_hi * 2 + y_lo), z: 8, core: 2. Of those that a mesh axis runs over, the one named last changes fastest.
Arguments:
- tokens: bfloat16 [32768, 3072], P(('dp', 'expert')), parts along dimension 0, may hold values from -6 to 6
- w_gate: bfloat16 [3072, 8192], P(None, 'expert'), may hold values from -0.109375 to 0.109375
- w_up: bfloat16 [3072, 8192], P(None, 'expert'), may hold values from -0.109375 to 0.109375
- w_down: bfloat16 [8192, 3072], P('expert'), may hold values from -0.0625 to 0.0625
- route_ids: int32 [32768, 2], P(('dp', 'expert')), parts along dimension 0, may hold values from 0 to 7, as said below
- route_prob: float32 [32768], P(('dp', 'expert')), parts along dimension 0, may hold values from 0.5 to 0.95
- slot_index: int32 [32768], P(('dp', 'expert')), parts along dimension 0, may hold values from 0 to 64, as said below
Outputs:
- mixed: bfloat16 [32768, 3072], P(('dp', 'expert')), parts along dimension 0
The draws below stay inside these ranges and needn't reach their ends.
There are 16 independent parts, one for each index of `dp`. The reference program is written for one: setup_inputs(seed, part) draws one part's arguments, and reference() takes and returns one part's arrays. A program takes and returns all parts, laid end to end along the dimension named above; an argument that names none is the same for every part. Nothing has to cross between parts.
Inputs may be any that keep to these rules, and one draw needn't show every extreme that they name: `route_ids`: each row names two different experts. `slot_index`: a token of whose two experts one is expert 0 holds its rank, in row order, among the tokens of its device that name expert 0; every other token holds 64. At most 64 of one device's 128 tokens name expert 0, and some device has exactly 64; the router's capacity of 64 tokens for expert 0 is counted over each aligned pair of 256 tokens (blocks 2k and 2k + 1) and is always filled, so those two devices have exactly 64 such tokens together.
All inputs are finite; a program needn't handle non-finite values.
Results may differ from the reference program's by a relative error of at most 0.023.
Values may be sent and summed in bfloat16 or wider, within the bound.
No kernel may reach another device: no remote copies, remote signals or barrier semaphores. Data moves between devices by JAX's collectives and lax.ppermute only.
A program may use at most 128 MiB of HBM per device.

```python
import jax
import jax.numpy as jnp
from jax import lax

D = 3072
FF = 8192
NUM_EXPERTS = 8
TOK_DEV = 128
CAP = 64
TOKENS = 2048
N_EXPERT = 16


def routing_draw(key):
    base = jax.random.fold_in(key, 77)
    blocks = TOKENS // TOK_DEV
    pairs = blocks // 2
    capacity = TOK_DEV // 2
    streams = jax.random.split(base, 6)
    level = jax.random.randint(streams[0], (pairs,), 0, 4)
    fullest = jax.random.randint(streams[1], (), 0, pairs)
    level = jnp.where(jnp.arange(pairs) == fullest, 0, level)
    table = jnp.array([capacity, capacity // 2, capacity // 4, capacity // 8], jnp.int32)
    even_counts = table[level]
    counts = jnp.stack([even_counts, capacity - even_counts], axis=1).reshape(blocks)
    order = jax.vmap(lambda one_key: jax.random.permutation(one_key, TOK_DEV))(jax.random.split(streams[2], blocks))
    routed = order < counts[:, None]
    ranking = jnp.cumsum(routed.astype(jnp.int32), axis=1) - 1
    slots = jnp.where(routed, ranking, capacity).reshape(TOKENS).astype(jnp.int32)
    other = jax.random.randint(streams[3], (TOKENS,), 1, NUM_EXPERTS)
    offset = jax.random.randint(streams[4], (TOKENS,), 1, NUM_EXPERTS - 1)
    second = 1 + (other - 1 + offset) % (NUM_EXPERTS - 1)
    flipped = jax.random.randint(streams[5], (TOKENS,), 0, 2)
    flat_routed = routed.reshape(TOKENS)
    first_column = jnp.where(flat_routed, jnp.where(flipped == 1, 0, other), other)
    second_column = jnp.where(flat_routed, jnp.where(flipped == 1, other, 0), second)
    chosen = jnp.stack([first_column, second_column], axis=1).astype(jnp.int32)
    return (chosen, slots)


def draw_route_ids(key, part):
    chosen, slots = routing_draw(key)
    return chosen


def draw_slot_index(key, part):
    chosen, slots = routing_draw(key)
    return slots


def steps_of(rng, dims, shards, smallest, high):
    loudness = 1.0
    for axis_at, blocks in shards:
        steps = jax.random.uniform(jax.random.fold_in(jax.random.fold_in(rng, 6), axis_at), (blocks,), jnp.float32, smallest / len(shards), high / len(shards))
        loudness = loudness * jnp.repeat(jnp.exp(steps), dims[axis_at] // blocks).reshape((-1,) + (1,) * (len(dims) - 1 - axis_at))
    return loudness


def bell_draw(own_key, shape, width, reach, shards=(), kind=jnp.bfloat16):
    result = jax.random.normal(own_key, shape, jnp.float32) * width
    if len(shards) > 0:
        result = steps_of(own_key, shape, shards, -0.22, 0.18) * result
    return jnp.clip(result, min=-reach, max=reach).astype(kind)


def setup_inputs(seed: int = 0, part: int = 0) -> dict:
    streams_of = jax.random.split(jax.random.key(seed), 8)
    own_keys = jax.random.split(jax.random.fold_in(streams_of[7], part), 8)
    return {
        "tokens": bell_draw(own_keys[0], (TOKENS, D), 1.0, 6.0, ((0, 16),)),
        "w_gate": bell_draw(streams_of[1], (D, FF), D ** -0.5, 0.109375, ((1, 16),)),
        "w_up": bell_draw(streams_of[2], (D, FF), D ** -0.5, 0.109375, ((1, 16),)),
        "w_down": bell_draw(streams_of[3], (FF, D), FF ** -0.5, 0.0625, ((0, 16),)),
        "route_ids": draw_route_ids(jax.random.fold_in(jax.random.fold_in(streams_of[7], part), 71), part),
        "route_prob": jnp.clip(0.5 + 0.45 * jax.random.uniform(own_keys[5], (TOKENS,), jnp.float32) ** steps_of(own_keys[5], (TOKENS,), ((0, 16),), -0.2, 0.2), 0.5, 0.95),
        "slot_index": draw_slot_index(jax.random.fold_in(jax.random.fold_in(streams_of[7], part), 71), part),
    }


def reference(tokens, w_gate, w_up, w_down, route_ids, route_prob, slot_index):
    share = jnp.where(route_ids[:, 0] == 0, route_prob, jnp.where(route_ids[:, 1] == 0, 1.0 - route_prob, 0.0))
    share = jnp.where(slot_index < CAP, share, 0.0).astype(jnp.float32)
    gate = jnp.dot(tokens, w_gate, preferred_element_type=jnp.float32)
    up = jnp.dot(tokens, w_up, preferred_element_type=jnp.float32)
    hidden = (jax.nn.silu(gate) * up).astype(jnp.bfloat16)
    group_width = FF // N_EXPERT
    hidden_groups = jnp.transpose(hidden.reshape(TOKENS, N_EXPERT, group_width), (1, 0, 2))
    down_groups = w_down.reshape(N_EXPERT, group_width, D)

    def accumulate(total, pieces):
        partial_value = jnp.dot(pieces[0], pieces[1], preferred_element_type=jnp.float32).astype(jnp.bfloat16)
        partial_value = lax.optimization_barrier(partial_value)
        return total + partial_value.astype(jnp.float32), None

    start_total = jnp.zeros((TOKENS, D), jnp.float32)
    down, _ = lax.scan(accumulate, start_total, (hidden_groups, down_groups))
    return (share[:, None] * down).astype(jnp.bfloat16)
```

```python
import jax
import jax.numpy as jnp
from jax import lax
from jax.sharding import Mesh, PartitionSpec as P

AXES = ("y_hi", "x", "core", "y_lo", "z")
SIZES = (2, 4, 2, 2, 8)
NZ = 8
NY = 4


def along_z(value, step):
    return lax.ppermute(value, "z", [(i, (i + step) % NZ) for i in range(NZ)])


def along_y(value, step):
    def index(y, core):
        return ((y // 2) * 2 + core) * 2 + y % 2

    pairs = [
        (index(y, core), index((y + (step if core == 0 else -step)) % NY, core)) for y in range(NY) for core in range(2)
    ]
    return lax.ppermute(value, ("y_hi", "core", "y_lo"), pairs)


def swap_pair(value):
    return lax.ppermute(value, "z", [(i, i ^ 1) for i in range(NZ)])


def expert(rows, w_gate, w_up, w_down):
    gate = jnp.dot(rows, w_gate, preferred_element_type=jnp.float32)
    up = jnp.dot(rows, w_up, preferred_element_type=jnp.float32)
    hidden = (jax.nn.silu(gate) * up).astype(jnp.bfloat16)
    return jnp.dot(hidden, w_down, preferred_element_type=jnp.float32).astype(jnp.bfloat16)


def total(*terms):
    value = terms[0].astype(jnp.float32)
    for term in terms[1:]:
        value = value + term.astype(jnp.float32)
    return value.astype(jnp.bfloat16)


together = lax.optimization_barrier


def shards(tokens, w_gate, w_up, w_down, route_ids, route_prob, slot_index):
    capacity = tokens.shape[0] // 2
    half = capacity // 2
    quarter = half // 2
    share = jnp.where(
        route_ids[:, 0] == 0, route_prob, jnp.where(route_ids[:, 1] == 0, 1.0 - route_prob, 0.0)
    )
    share = jnp.where(slot_index < capacity, share, 0.0)

    odd = lax.axis_index("z") % 2
    row = jnp.where(odd == 1, capacity - 1 - slot_index, slot_index)
    row = jnp.where(slot_index < capacity, row, -capacity)
    kept_row = row - odd * half
    sent_row = row - (1 - odd) * half
    lanes = jnp.arange(half, dtype=jnp.int32)[:, None]
    keep = (kept_row[None, :] == lanes).astype(jnp.bfloat16)
    send = (sent_row[None, :] == lanes).astype(jnp.bfloat16)
    arrived = swap_pair(jnp.dot(send, tokens, preferred_element_type=jnp.float32).astype(jnp.bfloat16))
    kept = jnp.dot(keep, tokens, preferred_element_type=jnp.float32).astype(jnp.bfloat16)
    own = arrived + kept

    up1, down1 = along_z(own, 1), along_z(own, -1)
    up1, down1 = together((up1, down1))
    up2, down2 = along_z(up1, 1), along_z(down1, -1)
    y1 = along_y(jnp.concatenate([own, up1, down1]), 1)
    up2, down2 = together((up2, down2))
    up3, down3 = along_z(up2, 1), along_z(down2, -1)
    y2 = along_y(jnp.concatenate([up2, down2]), 1)
    up3, down3, y1 = together((up3, down3, y1))
    up4, down4 = along_z(up3[:quarter], 1), along_z(down3[quarter:], -1)
    y3 = along_y(jnp.concatenate([up3, down3]), 1)
    up4, down4, y2 = together((up4, down4, y2))
    y4 = along_y(jnp.concatenate([up4, down4]), 1)

    mine = jnp.concatenate([own, up1, down1, up2, down2, up3, down3, up4, down4])
    mine_out = expert(mine, w_gate, w_up, w_down)
    mine_out, y4 = together((mine_out, y4))
    theirs = jnp.concatenate([y1, y2, y3, y4])
    theirs_out = expert(theirs, w_gate, w_up, w_down)

    def piece(value, c, count=1):
        return value[c * half : (c + count) * half]

    b4 = along_y(piece(theirs_out, 7), -1)
    t4 = total(piece(mine_out, 7), b4)
    b3 = along_y(piece(theirs_out, 5, 2), -1)
    f_down, f_up = along_z(t4[:quarter], -1), along_z(t4[quarter:], 1)
    f_down, f_up, b3 = together((f_down, f_up, b3))
    zero = jnp.zeros_like(f_down)
    f_down, f_up = jnp.concatenate([f_down, zero]), jnp.concatenate([zero, f_up])
    t_down = total(piece(mine_out, 5), b3[:half], f_down)
    t_up = total(piece(mine_out, 6), b3[half:], f_up)
    t_down, t_up = together((t_down, t_up))
    b2 = along_y(piece(theirs_out, 3, 2), -1)
    f_down, f_up = along_z(t_down, -1), along_z(t_up, 1)
    f_down, f_up, b2 = together((f_down, f_up, b2))
    t_down = total(piece(mine_out, 3), b2[:half], f_down)
    t_up = total(piece(mine_out, 4), b2[half:], f_up)
    t_down, t_up = together((t_down, t_up))
    b1 = along_y(piece(theirs_out, 0, 3), -1)
    f_down, f_up = along_z(t_down, -1), along_z(t_up, 1)
    f_down, f_up, b1 = together((f_down, f_up, b1))
    t_down = total(piece(mine_out, 1), b1[half : 2 * half], f_down)
    t_up = total(piece(mine_out, 2), b1[2 * half :], f_up)
    t_down, t_up = together((t_down, t_up))
    f_down, f_up = along_z(t_down, -1), along_z(t_up, 1)
    down_own = total(piece(mine_out, 0), b1[:half], f_down, f_up)

    down_other = swap_pair(down_own)
    placed = jnp.einsum("cr,cd->rd", keep, down_own, preferred_element_type=jnp.float32)
    placed = placed + jnp.einsum("cr,cd->rd", send, down_other, preferred_element_type=jnp.float32)
    return (share[:, None] * placed).astype(jnp.bfloat16)


def solution(mesh):
    fine = Mesh(mesh.devices.reshape(SIZES), AXES)
    every = ("y_hi", "x", "core", "y_lo", "z")
    group = ("y_lo", "z")
    return jax.shard_map(
        shards,
        mesh=fine,
        in_specs=(
            P(every, None),
            P(None, group),
            P(None, group),
            P(group, None),
            P(every, None),
            P(every),
            P(every),
        ),
        out_specs=P(every, None),
        check_vma=False,
    )
```

```python
import functools

import jax
import jax.numpy as jnp
from jax import lax
from jax.experimental import pallas as pl
from jax.experimental.pallas import tpu as pltpu
from jax.sharding import Mesh, PartitionSpec as P

AXES = ("y_hi", "x", "core", "y_lo", "z")
SIZES = (2, 4, 2, 2, 8)
NZ = 8
NY = 4


def along_z(value, step):
    def index(core, z):
        return core * NZ + z

    pairs = [
        (index(core, z), index(core, (z + (step if core == 0 else -step)) % NZ)) for core in range(2) for z in range(NZ)
    ]
    return lax.ppermute(value, ("core", "z"), pairs)


def along_y(value, step):
    def index(y, core):
        return ((y // 2) * 2 + core) * 2 + y % 2

    pairs = [
        (index(y, core), index((y + (step if core == 0 else -step)) % NY, core)) for y in range(NY) for core in range(2)
    ]
    return lax.ppermute(value, ("y_hi", "core", "y_lo"), pairs)


def swap_pair(value):
    return lax.ppermute(value, "z", [(i, i ^ 1) for i in range(NZ)])


def diagonal(value, step_y, step_z):
    def index(y, core, z):
        return (((y // 2) * 2 + core) * 2 + y % 2) * NZ + z

    pairs = [
        (index(y, core, z), index((y + (step_y if core == 0 else -step_y)) % NY, core, (z + (step_z if core == 0 else -step_z)) % NZ))
        for y in range(NY)
        for core in range(2)
        for z in range(NZ)
    ]
    return lax.ppermute(value, ("y_hi", "core", "y_lo", "z"), pairs)


def expert_kernel(count, *refs):
    pieces, (w_gate, w_up, w_down) = refs[:count], refs[count : count + 3]
    outs, (rows, hidden) = refs[count + 3 : 2 * count + 3], refs[2 * count + 3 :]
    at = 0
    for piece in pieces:
        rows[pl.ds(at, piece.shape[0]), :] = piece[...]
        at += piece.shape[0]
    inner, width = w_down.shape
    for start in range(0, inner, 256):
        stop = min(start + 256, inner)
        gate = jnp.dot(rows[...], w_gate[:, start:stop], preferred_element_type=jnp.float32)
        up = jnp.dot(rows[...], w_up[:, start:stop], preferred_element_type=jnp.float32)
        hidden[:, start:stop] = (gate / (1.0 + jnp.exp(-gate)) * up).astype(hidden.dtype)
    for start in range(0, width, 512):
        stop = min(start + 512, width)
        part = jnp.dot(hidden[...], w_down[:, start:stop], preferred_element_type=jnp.float32)
        part = part.astype(hidden.dtype)
        at = 0
        for out in outs:
            out[:, start:stop] = part[at : at + out.shape[0]]
            at += out.shape[0]


def fetch_kernel(*refs):
    count = len(refs) // 3
    copies = [pltpu.make_async_copy(*refs[i::count]) for i in range(count)]
    for copy in copies:
        copy.start()
    for copy in copies:
        copy.wait()


def fetch(*arrays):
    count = len(arrays)
    return pl.pallas_call(
        fetch_kernel,
        out_shape=[pltpu.VMEM(v.shape, v.dtype) for v in arrays],
        in_specs=[pl.BlockSpec(memory_space=pltpu.HBM)] * count,
        out_specs=[pl.BlockSpec(memory_space=pltpu.VMEM)] * count,
        scratch_shapes=[pltpu.SemaphoreType.DMA] * count,
        compiler_params=pltpu.CompilerParams(vmem_limit_bytes=1024 * 1024),
        cost_estimate=pl.CostEstimate(
            flops=0, transcendentals=0, bytes_accessed=sum(v.size * v.dtype.itemsize for v in arrays)
        ),
    )(*[pltpu.with_memory_space_constraint(v, pltpu.HBM) for v in arrays])


def expert(pieces, w_gate, w_up, w_down):
    count = len(pieces)
    total_rows = sum(p.shape[0] for p in pieces)
    inner, width = w_down.shape
    vmem = lambda n: [pl.BlockSpec(memory_space=pltpu.VMEM)] * n
    operands = [pltpu.with_memory_space_constraint(v, pltpu.VMEM) for v in (*pieces, w_gate, w_up, w_down)]
    return pl.pallas_call(
        functools.partial(expert_kernel, count),
        out_shape=[pltpu.VMEM(p.shape, p.dtype) for p in pieces],
        in_specs=vmem(count + 3),
        out_specs=vmem(count),
        scratch_shapes=[
            pltpu.VMEM((total_rows, width), jnp.bfloat16),
            pltpu.VMEM((total_rows, inner), jnp.bfloat16),
        ],
        compiler_params=pltpu.CompilerParams(vmem_limit_bytes=8 * 1024 * 1024),
        cost_estimate=pl.CostEstimate(
            flops=6 * total_rows * inner * width,
            transcendentals=total_rows * inner,
            bytes_accessed=6 * inner * width,
        ),
    )(*operands)


def total(*terms):
    value = terms[0].astype(jnp.float32)
    for term in terms[1:]:
        value = value + term.astype(jnp.float32)
    return value.astype(jnp.bfloat16)


together = lax.optimization_barrier


def shards(tokens, w_gate, w_up, w_down, route_ids, route_prob, slot_index):
    capacity = tokens.shape[0] // 2
    half = capacity // 2
    share = jnp.where(
        route_ids[:, 0] == 0, route_prob, jnp.where(route_ids[:, 1] == 0, 1.0 - route_prob, 0.0)
    )
    share = jnp.where(slot_index < capacity, share, 0.0)

    odd = lax.axis_index("z") % 2
    row = jnp.where(odd == 1, capacity - 1 - slot_index, slot_index)
    row = jnp.where(slot_index < capacity, row, -capacity)
    kept_row = row - odd * half
    sent_row = row - (1 - odd) * half
    lanes = jnp.arange(half, dtype=jnp.int32)[:, None]
    keep = (kept_row[None, :] == lanes).astype(jnp.bfloat16)
    send = (sent_row[None, :] == lanes).astype(jnp.bfloat16)
    sent = jnp.dot(send, tokens, preferred_element_type=jnp.float32).astype(jnp.bfloat16)
    arrived = swap_pair(sent)
    kept = jnp.dot(keep, tokens, preferred_element_type=jnp.float32).astype(jnp.bfloat16)
    arrived, kept = together((arrived, kept))
    own = arrived + kept

    up1, down1 = along_z(own, 1), along_z(own, -1)
    weights = fetch(w_gate, w_up, w_down)
    up1, down1, weights = together((up1, down1, weights))
    up2, down2 = along_z(up1, 1), along_z(down1, -1)
    y1 = along_y(jnp.concatenate([own, up1, down1]), 1)
    up2, down2 = together((up2, down2))
    up3, down3 = along_z(up2, 1), along_z(down2, -1)
    y2 = along_y(jnp.concatenate([up2, down2]), 1)
    up3, down3, y1 = together((up3, down3, y1))
    up4, y4 = along_z(up3, 1), diagonal(up3, 1, 1)
    y3 = along_y(jnp.concatenate([up3, down3]), 1)
    y2, *mine = together((y2, own, up1, down1, up2, down2, up3, down3))
    *mine, o1, o2 = expert([*mine, y1, y2], *weights)
    mine, up4, y3, y4 = together((mine, up4, y3, y4))
    m4, o3, o4 = expert([up4, y3, y4], *weights)

    f_down, g_down = along_z(m4, -1), diagonal(o4, -1, -1)
    b3 = along_y(o3, -1)
    f_down, g_down, b3 = together((f_down, g_down, b3))
    t_down = total(mine[5], b3[:half], f_down, g_down)
    t_up = total(mine[6], b3[half:])
    t_down, t_up = together((t_down, t_up))
    b2 = along_y(o2, -1)
    f_down, f_up = along_z(t_down, -1), along_z(t_up, 1)
    f_down, f_up, b2 = together((f_down, f_up, b2))
    t_down = total(mine[3], b2[:half], f_down)
    t_up = total(mine[4], b2[half:], f_up)
    t_down, t_up = together((t_down, t_up))
    b1 = along_y(o1, -1)
    f_down, f_up = along_z(t_down, -1), along_z(t_up, 1)
    f_down, f_up, b1 = together((f_down, f_up, b1))
    t_down = total(mine[1], b1[half : 2 * half], f_down)
    t_up = total(mine[2], b1[2 * half :], f_up)
    t_down, t_up = together((t_down, t_up))
    f_down, f_up = along_z(t_down, -1), along_z(t_up, 1)
    down_own = total(mine[0], b1[:half], f_down, f_up)

    down_other = swap_pair(down_own)
    placed = jnp.einsum("cr,cd->rd", keep, down_own, preferred_element_type=jnp.float32)
    placed = placed + jnp.einsum("cr,cd->rd", send, down_other, preferred_element_type=jnp.float32)
    return (share[:, None] * placed).astype(jnp.bfloat16)


def solution(mesh):
    fine = Mesh(mesh.devices.reshape(SIZES), AXES)
    every = ("y_hi", "x", "core", "y_lo", "z")
    group = ("y_lo", "z")
    return jax.shard_map(
        shards,
        mesh=fine,
        in_specs=(
            P(every, None),
            P(None, group),
            P(None, group),
            P(group, None),
            P(every, None),
            P(every),
            P(every),
        ),
        out_specs=P(every, None),
        check_vma=False,
    )
```

```python
import functools

import jax
import jax.numpy as jnp
from jax import lax
from jax.experimental import pallas as pl
from jax.experimental.pallas import tpu as pltpu
from jax.sharding import Mesh, PartitionSpec as P

AXES = ("y_hi", "x", "core", "y_lo", "z")
SIZES = (2, 4, 2, 2, 8)
NZ = 8
NY = 4


def along_z(value, step):
    return lax.ppermute(value, "z", [(i, (i + step) % NZ) for i in range(NZ)])


def along_z_by_core(value, step):
    def index(core, z):
        return core * NZ + z

    pairs = [
        (index(core, z), index(core, (z + (step if core == 0 else -step)) % NZ)) for core in range(2) for z in range(NZ)
    ]
    return lax.ppermute(value, ("core", "z"), pairs)


def along_y(value, step):
    def index(y, core):
        return ((y // 2) * 2 + core) * 2 + y % 2

    pairs = [
        (index(y, core), index((y + (step if core == 0 else -step)) % NY, core)) for y in range(NY) for core in range(2)
    ]
    return lax.ppermute(value, ("y_hi", "core", "y_lo"), pairs)


def swap_pair(value):
    return lax.ppermute(value, "z", [(i, i ^ 1) for i in range(NZ)])


def diagonal(value, step_y, step_z):
    def index(y, core, z):
        return (((y // 2) * 2 + core) * 2 + y % 2) * NZ + z

    pairs = [
        (index(y, core, z), index((y + (step_y if core == 0 else -step_y)) % NY, core, (z + (step_z if core == 0 else -step_z)) % NZ))
        for y in range(NY)
        for core in range(2)
        for z in range(NZ)
    ]
    return lax.ppermute(value, ("y_hi", "core", "y_lo", "z"), pairs)


def expert_kernel(count, *refs):
    pieces, (w_gate, w_up, w_down) = refs[:count], refs[count : count + 3]
    outs, (rows, hidden) = refs[count + 3 : 2 * count + 3], refs[2 * count + 3 :]
    at = 0
    for piece in pieces:
        rows[pl.ds(at, piece.shape[0]), :] = piece[...]
        at += piece.shape[0]
    inner, width = w_down.shape
    for start in range(0, inner, 256):
        stop = min(start + 256, inner)
        gate = jnp.dot(rows[...], w_gate[:, start:stop], preferred_element_type=jnp.float32)
        up = jnp.dot(rows[...], w_up[:, start:stop], preferred_element_type=jnp.float32)
        hidden[:, start:stop] = (gate / (1.0 + jnp.exp(-gate)) * up).astype(hidden.dtype)
    for start in range(0, width, 512):
        stop = min(start + 512, width)
        part = jnp.dot(hidden[...], w_down[:, start:stop], preferred_element_type=jnp.float32)
        part = part.astype(hidden.dtype)
        at = 0
        for out in outs:
            out[:, start:stop] = part[at : at + out.shape[0]]
            at += out.shape[0]


def fetch_kernel(*refs):
    count = len(refs) // 3
    copies = [pltpu.make_async_copy(*refs[i::count]) for i in range(count)]
    for copy in copies:
        copy.start()
    for copy in copies:
        copy.wait()


def fetch(*arrays):
    count = len(arrays)
    return pl.pallas_call(
        fetch_kernel,
        out_shape=[pltpu.VMEM(v.shape, v.dtype) for v in arrays],
        in_specs=[pl.BlockSpec(memory_space=pltpu.HBM)] * count,
        out_specs=[pl.BlockSpec(memory_space=pltpu.VMEM)] * count,
        scratch_shapes=[pltpu.SemaphoreType.DMA] * count,
        compiler_params=pltpu.CompilerParams(vmem_limit_bytes=1024 * 1024),
        cost_estimate=pl.CostEstimate(
            flops=0, transcendentals=0, bytes_accessed=sum(v.size * v.dtype.itemsize for v in arrays)
        ),
    )(*[pltpu.with_memory_space_constraint(v, pltpu.HBM) for v in arrays])


def expert(pieces, w_gate, w_up, w_down):
    count = len(pieces)
    total_rows = sum(p.shape[0] for p in pieces)
    inner, width = w_down.shape
    vmem = lambda n: [pl.BlockSpec(memory_space=pltpu.VMEM)] * n
    operands = [pltpu.with_memory_space_constraint(v, pltpu.VMEM) for v in (*pieces, w_gate, w_up, w_down)]
    return pl.pallas_call(
        functools.partial(expert_kernel, count),
        out_shape=[pltpu.VMEM(p.shape, p.dtype) for p in pieces],
        in_specs=vmem(count + 3),
        out_specs=vmem(count),
        scratch_shapes=[
            pltpu.VMEM((total_rows, width), jnp.bfloat16),
            pltpu.VMEM((total_rows, inner), jnp.bfloat16),
        ],
        compiler_params=pltpu.CompilerParams(vmem_limit_bytes=8 * 1024 * 1024),
        cost_estimate=pl.CostEstimate(
            flops=6 * total_rows * inner * width,
            transcendentals=total_rows * inner,
            bytes_accessed=6 * inner * width,
        ),
    )(*operands)


def total(*terms):
    value = terms[0].astype(jnp.float32)
    for term in terms[1:]:
        value = value + term.astype(jnp.float32)
    return value.astype(jnp.bfloat16)


together = lax.optimization_barrier


def shards(tokens, w_gate, w_up, w_down, route_ids, route_prob, slot_index):
    capacity = tokens.shape[0] // 2
    half = capacity // 2
    share = jnp.where(
        route_ids[:, 0] == 0, route_prob, jnp.where(route_ids[:, 1] == 0, 1.0 - route_prob, 0.0)
    )
    share = jnp.where(slot_index < capacity, share, 0.0)

    odd = lax.axis_index("z") % 2
    row = jnp.where(odd == 1, capacity - 1 - slot_index, slot_index)
    row = jnp.where(slot_index < capacity, row, -capacity)
    kept_row = row - odd * half
    sent_row = row - (1 - odd) * half
    lanes = jnp.arange(half, dtype=jnp.int32)[:, None]
    keep = (kept_row[None, :] == lanes).astype(jnp.bfloat16)
    send = (sent_row[None, :] == lanes).astype(jnp.bfloat16)
    sent = jnp.dot(send, tokens, preferred_element_type=jnp.float32).astype(jnp.bfloat16)
    arrived = swap_pair(sent)
    kept = jnp.dot(keep, tokens, preferred_element_type=jnp.float32).astype(jnp.bfloat16)
    arrived, kept = together((arrived, kept))
    own = arrived + kept

    first = lax.axis_index("core") == 0
    up1, down1 = along_z(own, 1), along_z(own, -1)
    weights = fetch(w_gate, w_up, w_down)
    down1, weights = together((down1, weights))
    up2, down2 = along_z(up1, 1), along_z(down1, -1)
    y1 = along_y(jnp.concatenate([own, up1, down1]), 1)
    up3, down3 = along_z(up2, 1), along_z(down2, -1)
    y2 = along_y(jnp.concatenate([up2, down2]), 1)
    last = jnp.where(first, up3, down3)
    far, y4 = along_z_by_core(last, 1), diagonal(last, 1, 1)
    y3 = along_y(jnp.concatenate([up3, down3]), 1)
    y1, y2, *mine = together((y1, y2, own, up1, down1, up2, down2, up3, down3))
    *mine, o1, o2 = expert([*mine, y1, y2], *weights)
    mine, far, y3, y4 = together((mine, far, y3, y4))
    m4, o3, o4 = expert([far, y3, y4], *weights)

    f, g = along_z_by_core(m4, -1), diagonal(o4, -1, -1)
    b3 = along_y(o3, -1)
    f, g, b3 = together((f, g, b3))
    t_down = total(mine[5], b3[:half], jnp.where(first, f, 0), jnp.where(first, g, 0))
    t_up = total(mine[6], b3[half:], jnp.where(first, 0, f), jnp.where(first, 0, g))
    t_down, t_up = together((t_down, t_up))
    b2 = along_y(o2, -1)
    f_down, f_up = along_z(t_down, -1), along_z(t_up, 1)
    f_down, f_up, b2 = together((f_down, f_up, b2))
    t_down = total(mine[3], b2[:half], f_down)
    t_up = total(mine[4], b2[half:], f_up)
    t_down, t_up = together((t_down, t_up))
    b1 = along_y(o1, -1)
    f_down, f_up = along_z(t_down, -1), along_z(t_up, 1)
    f_down, f_up, b1 = together((f_down, f_up, b1))
    t_down = total(mine[1], b1[half : 2 * half], f_down)
    t_up = total(mine[2], b1[2 * half :], f_up)
    t_down, t_up = together((t_down, t_up))
    f_down, f_up = along_z(t_down, -1), along_z(t_up, 1)
    down_own = total(mine[0], b1[:half], f_down, f_up)

    down_other = swap_pair(down_own)
    placed = jnp.einsum("cr,cd->rd", keep, down_own, preferred_element_type=jnp.float32)
    down_other, placed = together((down_other, placed))
    placed = placed + jnp.einsum("cr,cd->rd", send, down_other, preferred_element_type=jnp.float32)
    return (share[:, None] * placed).astype(jnp.bfloat16)


def solution(mesh):
    fine = Mesh(mesh.devices.reshape(SIZES), AXES)
    every = ("y_hi", "x", "core", "y_lo", "z")
    group = ("y_lo", "z")
    return jax.shard_map(
        shards,
        mesh=fine,
        in_specs=(
            P(every, None),
            P(None, group),
            P(None, group),
            P(group, None),
            P(every, None),
            P(every),
            P(every),
        ),
        out_specs=P(every, None),
        check_vma=False,
    )
```

```python
import functools

import jax
import jax.numpy as jnp
from jax import lax
from jax.experimental import pallas as pl
from jax.experimental.pallas import tpu as pltpu
from jax.sharding import Mesh, PartitionSpec as P

AXES = ("y_hi", "x", "core", "y_lo", "z")
SIZES = (2, 4, 2, 2, 8)
NZ = 8
NY = 4


def along_z(value, step):
    return lax.ppermute(value, "z", [(i, (i + step) % NZ) for i in range(NZ)])


def along_y(value, step):
    def index(y, core):
        return ((y // 2) * 2 + core) * 2 + y % 2

    pairs = [
        (index(y, core), index((y + (step if core == 0 else -step)) % NY, core)) for y in range(NY) for core in range(2)
    ]
    return lax.ppermute(value, ("y_hi", "core", "y_lo"), pairs)


def swap_pair(value):
    return lax.ppermute(value, "z", [(i, i ^ 1) for i in range(NZ)])


def diagonal(value, step_y, step_z):
    def index(y, core, z):
        return (((y // 2) * 2 + core) * 2 + y % 2) * NZ + z

    pairs = [
        (index(y, core, z), index((y + (step_y if core == 0 else -step_y)) % NY, core, (z + step_z) % NZ))
        for y in range(NY)
        for core in range(2)
        for z in range(NZ)
    ]
    return lax.ppermute(value, ("y_hi", "core", "y_lo", "z"), pairs)


def expert_kernel(count, *refs):
    pieces, (w_gate, w_up, w_down) = refs[:count], refs[count : count + 3]
    outs, (rows, hidden) = refs[count + 3 : 2 * count + 3], refs[2 * count + 3 :]
    at = 0
    for piece in pieces:
        rows[pl.ds(at, piece.shape[0]), :] = piece[...]
        at += piece.shape[0]
    inner, width = w_down.shape
    for start in range(0, inner, 256):
        stop = min(start + 256, inner)
        gate = jnp.dot(rows[...], w_gate[:, start:stop], preferred_element_type=jnp.float32)
        up = jnp.dot(rows[...], w_up[:, start:stop], preferred_element_type=jnp.float32)
        hidden[:, start:stop] = (gate / (1.0 + jnp.exp(-gate)) * up).astype(hidden.dtype)
    for start in range(0, width, 512):
        stop = min(start + 512, width)
        part = jnp.dot(hidden[...], w_down[:, start:stop], preferred_element_type=jnp.float32)
        part = part.astype(hidden.dtype)
        at = 0
        for out in outs:
            out[:, start:stop] = part[at : at + out.shape[0]]
            at += out.shape[0]


def fetch_kernel(*refs):
    count = len(refs) // 3
    copies = [pltpu.make_async_copy(*refs[i::count]) for i in range(count)]
    for copy in copies:
        copy.start()
    for copy in copies:
        copy.wait()


def fetch(*arrays):
    count = len(arrays)
    return pl.pallas_call(
        fetch_kernel,
        out_shape=[pltpu.VMEM(v.shape, v.dtype) for v in arrays],
        in_specs=[pl.BlockSpec(memory_space=pltpu.HBM)] * count,
        out_specs=[pl.BlockSpec(memory_space=pltpu.VMEM)] * count,
        scratch_shapes=[pltpu.SemaphoreType.DMA] * count,
        compiler_params=pltpu.CompilerParams(vmem_limit_bytes=1024 * 1024),
        cost_estimate=pl.CostEstimate(
            flops=0, transcendentals=0, bytes_accessed=sum(v.size * v.dtype.itemsize for v in arrays)
        ),
    )(*[pltpu.with_memory_space_constraint(v, pltpu.HBM) for v in arrays])


def expert(pieces, w_gate, w_up, w_down):
    count = len(pieces)
    total_rows = sum(p.shape[0] for p in pieces)
    inner, width = w_down.shape
    vmem = lambda n: [pl.BlockSpec(memory_space=pltpu.VMEM)] * n
    operands = [pltpu.with_memory_space_constraint(v, pltpu.VMEM) for v in (*pieces, w_gate, w_up, w_down)]
    return pl.pallas_call(
        functools.partial(expert_kernel, count),
        out_shape=[pltpu.VMEM(p.shape, p.dtype) for p in pieces],
        in_specs=vmem(count + 3),
        out_specs=vmem(count),
        scratch_shapes=[
            pltpu.VMEM((total_rows, width), jnp.bfloat16),
            pltpu.VMEM((total_rows, inner), jnp.bfloat16),
        ],
        compiler_params=pltpu.CompilerParams(vmem_limit_bytes=8 * 1024 * 1024),
        cost_estimate=pl.CostEstimate(
            flops=6 * total_rows * inner * width,
            transcendentals=total_rows * inner,
            bytes_accessed=6 * inner * width,
        ),
    )(*operands)


def total(*terms):
    value = terms[0].astype(jnp.float32)
    for term in terms[1:]:
        value = value + term.astype(jnp.float32)
    return value.astype(jnp.bfloat16)


together = lax.optimization_barrier


def shards(tokens, w_gate, w_up, w_down, route_ids, route_prob, slot_index):
    capacity = tokens.shape[0] // 2
    half = capacity // 2
    share = jnp.where(
        route_ids[:, 0] == 0, route_prob, jnp.where(route_ids[:, 1] == 0, 1.0 - route_prob, 0.0)
    )
    share = jnp.where(slot_index < capacity, share, 0.0)

    odd = lax.axis_index("z") % 2
    row = jnp.where(odd == 1, capacity - 1 - slot_index, slot_index)
    row = jnp.where(slot_index < capacity, row, -capacity)
    kept_row = row - odd * half
    sent_row = row - (1 - odd) * half
    lanes = jnp.arange(half, dtype=jnp.int32)[:, None]
    keep = (kept_row[None, :] == lanes).astype(jnp.bfloat16)
    send = (sent_row[None, :] == lanes).astype(jnp.bfloat16)
    sent = jnp.dot(send, tokens, preferred_element_type=jnp.float32).astype(jnp.bfloat16)
    arrived = swap_pair(sent)
    kept = jnp.dot(keep, tokens, preferred_element_type=jnp.float32).astype(jnp.bfloat16)
    arrived, kept = together((arrived, kept))
    own = arrived + kept

    up1, down1 = along_z(own, 1), along_z(own, -1)
    weights = fetch(w_gate, w_up, w_down)
    down1, weights = together((down1, weights))
    up2, down2 = along_z(up1, 1), along_z(down1, -1)
    y1 = along_y(jnp.concatenate([own, up1, down1]), 1)
    up3, down3 = along_z(up2, 1), along_z(down2, -1)
    y2 = along_y(jnp.concatenate([up2, down2]), 1)
    far, y4 = along_z(up3, 1), diagonal(down3, 1, -1)
    y3 = along_y(jnp.concatenate([up3, down3]), 1)
    y1, y2, *mine = together((y1, y2, own, up1, down1, up2, down2, up3, down3))
    *mine, o1, o2 = expert([*mine, y1, y2], *weights)
    mine, far, y3, y4 = together((mine, far, y3, y4))
    m4, o3, o4 = expert([far, y3, y4], *weights)

    f_down, f_up = along_z(m4, -1), diagonal(o4, -1, 1)
    b3 = along_y(o3, -1)
    f_down, f_up, b3 = together((f_down, f_up, b3))
    t_down = total(mine[5], b3[:half], f_down)
    t_up = total(mine[6], b3[half:], f_up)
    t_down, t_up = together((t_down, t_up))
    b2 = along_y(o2, -1)
    f_down, f_up = along_z(t_down, -1), along_z(t_up, 1)
    f_down, f_up, b2 = together((f_down, f_up, b2))
    t_down = total(mine[3], b2[:half], f_down)
    t_up = total(mine[4], b2[half:], f_up)
    t_down, t_up = together((t_down, t_up))
    b1 = along_y(o1, -1)
    f_down, f_up = along_z(t_down, -1), along_z(t_up, 1)
    f_down, f_up, b1 = together((f_down, f_up, b1))
    t_down = total(mine[1], b1[half : 2 * half], f_down)
    t_up = total(mine[2], b1[2 * half :], f_up)
    t_down, t_up = together((t_down, t_up))
    f_down, f_up = along_z(t_down, -1), along_z(t_up, 1)
    down_own = total(mine[0], b1[:half], f_down, f_up)

    down_other = swap_pair(down_own)
    placed = jnp.einsum("cr,cd->rd", keep, down_own, preferred_element_type=jnp.float32)
    down_other, placed = together((down_other, placed))
    placed = placed + jnp.einsum("cr,cd->rd", send, down_other, preferred_element_type=jnp.float32)
    return (share[:, None] * placed).astype(jnp.bfloat16)


def solution(mesh):
    fine = Mesh(mesh.devices.reshape(SIZES), AXES)
    every = ("y_hi", "x", "core", "y_lo", "z")
    group = ("y_lo", "z")
    return jax.shard_map(
        shards,
        mesh=fine,
        in_specs=(
            P(every, None),
            P(None, group),
            P(None, group),
            P(group, None),
            P(every, None),
            P(every),
            P(every),
        ),
        out_specs=P(every, None),
        check_vma=False,
    )
```

```python
import functools

import jax
import jax.numpy as jnp
from jax import lax
from jax.experimental import pallas as pl
from jax.experimental.pallas import tpu as pltpu
from jax.sharding import Mesh, PartitionSpec as P

AXES = ("y_hi", "x", "core", "y_lo", "z")
SIZES = (2, 4, 2, 2, 8)
NZ = 8
NY = 4


def along_z(value, step):
    return lax.ppermute(value, "z", [(i, (i + step) % NZ) for i in range(NZ)])


def along_y(value, step):
    def index(y, core):
        return ((y // 2) * 2 + core) * 2 + y % 2

    pairs = [
        (index(y, core), index((y + (step if core == 0 else -step)) % NY, core)) for y in range(NY) for core in range(2)
    ]
    return lax.ppermute(value, ("y_hi", "core", "y_lo"), pairs)


def swap_pair(value):
    return lax.ppermute(value, "z", [(i, i ^ 1) for i in range(NZ)])


def diagonal(value, step_y, step_z):
    def index(y, core, z):
        return (((y // 2) * 2 + core) * 2 + y % 2) * NZ + z

    pairs = [
        (index(y, core, z), index((y + (step_y if core == 0 else -step_y)) % NY, core, (z + step_z) % NZ))
        for y in range(NY)
        for core in range(2)
        for z in range(NZ)
    ]
    return lax.ppermute(value, ("y_hi", "core", "y_lo", "z"), pairs)


def expert_kernel(count, *refs):
    pieces, (w_gate, w_up, w_down) = refs[:count], refs[count : count + 3]
    outs, (rows, hidden) = refs[count + 3 : 2 * count + 3], refs[2 * count + 3 :]
    at = 0
    for piece in pieces:
        rows[pl.ds(at, piece.shape[0]), :] = piece[...]
        at += piece.shape[0]
    inner, width = w_down.shape
    for start in range(0, inner, 256):
        stop = min(start + 256, inner)
        gate = jnp.dot(rows[...], w_gate[:, start:stop], preferred_element_type=jnp.float32)
        up = jnp.dot(rows[...], w_up[:, start:stop], preferred_element_type=jnp.float32)
        hidden[:, start:stop] = (gate / (1.0 + jnp.exp(-gate)) * up).astype(hidden.dtype)
    for start in range(0, width, 512):
        stop = min(start + 512, width)
        part = jnp.dot(hidden[...], w_down[:, start:stop], preferred_element_type=jnp.float32)
        part = part.astype(hidden.dtype)
        at = 0
        for out in outs:
            out[:, start:stop] = part[at : at + out.shape[0]]
            at += out.shape[0]


def fetch_kernel(*refs):
    count = len(refs) // 3
    copies = [pltpu.make_async_copy(*refs[i::count]) for i in range(count)]
    for copy in copies:
        copy.start()
    for copy in copies:
        copy.wait()


def fetch(*arrays):
    count = len(arrays)
    return pl.pallas_call(
        fetch_kernel,
        out_shape=[pltpu.VMEM(v.shape, v.dtype) for v in arrays],
        in_specs=[pl.BlockSpec(memory_space=pltpu.HBM)] * count,
        out_specs=[pl.BlockSpec(memory_space=pltpu.VMEM)] * count,
        scratch_shapes=[pltpu.SemaphoreType.DMA] * count,
        compiler_params=pltpu.CompilerParams(vmem_limit_bytes=1024 * 1024),
        cost_estimate=pl.CostEstimate(
            flops=0, transcendentals=0, bytes_accessed=sum(v.size * v.dtype.itemsize for v in arrays)
        ),
    )(*[pltpu.with_memory_space_constraint(v, pltpu.HBM) for v in arrays])


def expert(pieces, w_gate, w_up, w_down):
    count = len(pieces)
    total_rows = sum(p.shape[0] for p in pieces)
    inner, width = w_down.shape
    vmem = lambda n: [pl.BlockSpec(memory_space=pltpu.VMEM)] * n
    operands = [pltpu.with_memory_space_constraint(v, pltpu.VMEM) for v in (*pieces, w_gate, w_up, w_down)]
    return pl.pallas_call(
        functools.partial(expert_kernel, count),
        out_shape=[pltpu.VMEM(p.shape, p.dtype) for p in pieces],
        in_specs=vmem(count + 3),
        out_specs=vmem(count),
        scratch_shapes=[
            pltpu.VMEM((total_rows, width), jnp.bfloat16),
            pltpu.VMEM((total_rows, inner), jnp.bfloat16),
        ],
        compiler_params=pltpu.CompilerParams(vmem_limit_bytes=8 * 1024 * 1024),
        cost_estimate=pl.CostEstimate(
            flops=6 * total_rows * inner * width,
            transcendentals=total_rows * inner,
            bytes_accessed=6 * inner * width,
        ),
    )(*operands)


def sum_kernel(half, at, mine, back, flow, out):
    value = mine[...].astype(jnp.float32) + back[at : at + half, :].astype(jnp.float32)
    out[...] = (value + flow[...].astype(jnp.float32)).astype(out.dtype)


def passed_on(mine, back, at, flow):
    operands = [pltpu.with_memory_space_constraint(v, pltpu.VMEM) for v in (mine, back, flow)]
    return pl.pallas_call(
        functools.partial(sum_kernel, mine.shape[0], at),
        out_shape=pltpu.VMEM(mine.shape, mine.dtype),
        in_specs=[pl.BlockSpec(memory_space=pltpu.VMEM)] * 3,
        out_specs=pl.BlockSpec(memory_space=pltpu.VMEM),
        compiler_params=pltpu.CompilerParams(vmem_limit_bytes=2 * 1024 * 1024),
        cost_estimate=pl.CostEstimate(flops=3 * mine.size, transcendentals=0, bytes_accessed=1024),
    )(*operands)


def total(*terms):
    value = terms[0].astype(jnp.float32)
    for term in terms[1:]:
        value = value + term.astype(jnp.float32)
    return value.astype(jnp.bfloat16)


together = lax.optimization_barrier


def shards(tokens, w_gate, w_up, w_down, route_ids, route_prob, slot_index):
    capacity = tokens.shape[0] // 2
    half = capacity // 2
    share = jnp.where(
        route_ids[:, 0] == 0, route_prob, jnp.where(route_ids[:, 1] == 0, 1.0 - route_prob, 0.0)
    )
    share = jnp.where(slot_index < capacity, share, 0.0)

    odd = lax.axis_index("z") % 2
    row = jnp.where(odd == 1, capacity - 1 - slot_index, slot_index)
    row = jnp.where(slot_index < capacity, row, -capacity)
    kept_row = row - odd * half
    sent_row = row - (1 - odd) * half
    lanes = jnp.arange(half, dtype=jnp.int32)[:, None]
    keep = (kept_row[None, :] == lanes).astype(jnp.bfloat16)
    send = (sent_row[None, :] == lanes).astype(jnp.bfloat16)
    sent = jnp.dot(send, tokens, preferred_element_type=jnp.float32).astype(jnp.bfloat16)
    arrived = swap_pair(sent)
    kept = jnp.dot(keep, tokens, preferred_element_type=jnp.float32).astype(jnp.bfloat16)
    arrived, kept = together((arrived, kept))
    own = arrived + kept

    up1, down1 = along_z(own, 1), along_z(own, -1)
    weights = fetch(w_gate, w_up, w_down)
    down1, weights = together((down1, weights))
    up2, down2 = along_z(up1, 1), along_z(down1, -1)
    y1 = along_y(jnp.concatenate([own, up1, down1]), 1)
    up3, down3 = along_z(up2, 1), along_z(down2, -1)
    y2 = along_y(jnp.concatenate([up2, down2]), 1)
    far, y4 = along_z(up3, 1), diagonal(down3, 1, -1)
    y3 = along_y(jnp.concatenate([up3, down3]), 1)
    y1, y2, *mine = together((y1, y2, own, up1, down1, up2, down2, up3, down3))
    *mine, o1, o2 = expert([*mine, y1, y2], *weights)
    mine, far, y3, y4 = together((mine, far, y3, y4))
    m4, o3, o4 = expert([far, y3, y4], *weights)

    f_down, f_up = along_z(m4, -1), diagonal(o4, -1, 1)
    b3 = along_y(o3, -1)
    f_down, f_up, b3 = together((f_down, f_up, b3))
    t_down = total(mine[5], b3[:half], f_down)
    t_up = total(mine[6], b3[half:], f_up)
    b2 = along_y(o2, -1)
    f_down, f_up = along_z(t_down, -1), along_z(t_up, 1)
    b1 = along_y(o1, -1)
    f_down = along_z(passed_on(mine[3], b2, 0, f_down), -1)
    f_up = along_z(passed_on(mine[4], b2, half, f_up), 1)
    f_down = along_z(passed_on(mine[1], b1, half, f_down), -1)
    f_up = along_z(passed_on(mine[2], b1, 2 * half, f_up), 1)
    down_own = total(mine[0], b1[:half], f_down, f_up)

    down_other = swap_pair(down_own)
    placed = jnp.einsum("cr,cd->rd", keep, down_own, preferred_element_type=jnp.float32)
    down_other, placed = together((down_other, placed))
    placed = placed + jnp.einsum("cr,cd->rd", send, down_other, preferred_element_type=jnp.float32)
    return (share[:, None] * placed).astype(jnp.bfloat16)


def solution(mesh):
    fine = Mesh(mesh.devices.reshape(SIZES), AXES)
    every = ("y_hi", "x", "core", "y_lo", "z")
    group = ("y_lo", "z")
    return jax.shard_map(
        shards,
        mesh=fine,
        in_specs=(
            P(every, None),
            P(None, group),
            P(None, group),
            P(group, None),
            P(every, None),
            P(every),
            P(every),
        ),
        out_specs=P(every, None),
        check_vma=False,
    )
```
